32 devices in a mesh: gx: 4 (over x, core), gy: 8 (over z, y).
Axes of the slice: x: 2, y: 2, z: 4, core: 2. Of those that a mesh axis runs over, the one named last changes fastest.
Arguments:
- farm_velocity: float32 [3, 64, 64, 192], P(None, 'gx', 'gy'), may hold values from -6 to 6
- precursor_velocity: float32 [3, 64, 64, 192], P(None, 'gx', 'gy'), may hold values from -6 to 6
- turb_cell: int32 [4, 8, 256], P('gx', 'gy'), may hold values from 0 to 24575
- turb_slot: int32 [4, 8, 256], P('gx', 'gy'), may hold values from 0 to 15
- disk_mask: int32 [4, 8, 256], P('gx', 'gy'), may hold values 0 or 1
Outputs:
- farm_new: float32 [3, 64, 64, 192], P(None, 'gx', 'gy')
- precursor_new: float32 [3, 64, 64, 192], P(None, 'gx', 'gy')
The draws below stay inside these ranges and needn't reach their ends.
Inputs may be any that keep to these rules, and one draw needn't show every extreme that they name: `turb_cell`: the cell is (x * 8 + y) * 192 + z within the device's tile of 16 x 8 x 192 cells.
All inputs are finite; a program needn't handle non-finite values. No bound on the sum of `disk_mask` on one device may be relied on, other than what follows from the above.
Results may differ from the reference program's by a relative error of at most 0.0003.
Values sent between devices are 32-bit elements; how exact they have to be, the bound alone decides.
A program may use at most 64 MiB of HBM per device.

```python
import math
import jax
import jax.numpy as jnp
from jax import lax

CX = 16
CY = 8
NZ = 192
NF = 48
TURB = 16
SLOTS = 256
NX = 64
NY = 64
N_GX = 4
N_GY = 8


def plant(values, own_key, smallest, top_value):
    longest = values.shape.index(max(values.shape))
    spots = []
    for shift in (0, 1):
        where = [jax.random.randint(jax.random.fold_in(own_key, axis), (), 0, length) for axis, length in enumerate(values.shape)]
        where[longest] = (where[longest] + shift) % values.shape[longest]
        spots.append(tuple(where))
    return values.at[spots[0]].set(smallest).at[spots[1]].set(top_value)


def levels(stream_key, shape, split, low, top_value):
    def one(position, parts):
        steps = jax.random.uniform(jax.random.fold_in(jax.random.fold_in(stream_key, 6), position), (parts,), jnp.float32, low / len(split), top_value / len(split))
        return jnp.repeat(jnp.exp(steps), shape[position] // parts).reshape((-1,) + (1,) * (len(shape) - position - 1))

    level = one(*split[0])
    for cut in split[1:]:
        level = level * one(*cut)
    return level


def noise(key, shape, spread, most, split=(), held_as=jnp.bfloat16):
    values = jax.random.normal(key, shape, jnp.float32) * spread
    if len(split) > 0:
        values = levels(key, shape, split, -0.22, 0.18) * values
    return jnp.clip(values, min=-most, max=most).astype(held_as)


def setup_inputs(seed: int = 0) -> dict:
    key_list = jax.random.split(jax.random.key(seed), 6)
    return {
        "farm_velocity": noise(key_list[0], (3, NX, NY, NZ), 1.0, 6.0, ((1, 4), (2, 8)), jnp.float32),
        "precursor_velocity": noise(key_list[1], (3, NX, NY, NZ), 1.0, 6.0, ((1, 4), (2, 8)), jnp.float32),
        "turb_cell": plant(jax.random.randint(key_list[2], (N_GX, N_GY, SLOTS), 0, CX * CY * NZ), jax.random.fold_in(key_list[2], 1), 0, (CX * CY * NZ) - 1).astype(jnp.int32),
        "turb_slot": plant(jax.random.randint(key_list[3], (N_GX, N_GY, SLOTS), 0, TURB), jax.random.fold_in(key_list[3], 1), 0, TURB - 1).astype(jnp.int32),
        "disk_mask": plant((jax.random.randint(key_list[4], (N_GX, N_GY, SLOTS), 0, 4) < 1).astype(jnp.int32), jax.random.fold_in(key_list[4], 1), 0, 1),
    }


WIND = 3.0
STEP = 0.1
SMAG = 0.0289
THRUST = 1.33
DIFFUSE = 0.05
HIGH = lax.Precision.HIGHEST

def inner(arr, axis, start, length):
    out = arr
    for dim in range(3):
        place = out.ndim - 3 + dim
        extent = arr.shape[arr.ndim - 3 + dim]
        if dim == axis:
            out = lax.slice_in_dim(out, start, start + length, axis=place)
        else:
            out = lax.slice_in_dim(out, 1, extent - 1, axis=place)
    return out

def farm_tendency(ext):
    padded = jnp.pad(ext, ((0, 0), (0, 0), (0, 0), (2, 2)))
    cycle = padded[:, 1:-1, 1:-1, 1:-1]
    grads = []
    for axis in range(3):
        extent = padded.shape[1 + axis]
        grads.append(0.5 * (inner(padded, axis, 2, extent - 2) - inner(padded, axis, 0, extent - 2)))
    square = jnp.zeros(cycle.shape[1:], jnp.float32)
    for first in range(3):
        for second in range(3):
            strain = 0.5 * (grads[second][first] + grads[first][second])
            square = square + strain * strain
    eddy = SMAG * jnp.sqrt(2.0 * square)
    advect = cycle + jnp.array([WIND, 0.0, 0.0], jnp.float32)[:, None, None, None]
    total = jnp.zeros((3,) + tuple((n - 2 for n in cycle.shape[1:])), jnp.float32)
    for axis in range(3):
        extent = cycle.shape[1 + axis]
        low_f = inner(cycle, axis, 0, extent - 1)
        high_f = inner(cycle, axis, 1, extent - 1)
        low_v = inner(advect[axis], axis, 0, extent - 1)
        high_v = inner(advect[axis], axis, 1, extent - 1)
        low_e = inner(eddy, axis, 0, extent - 1)
        high_e = inner(eddy, axis, 1, extent - 1)
        flux = 0.25 * (low_v + high_v) * (low_f + high_f) - 0.5 * (low_e + high_e) * (high_f - low_f)
        faces = extent - 1
        change = lax.slice_in_dim(flux, 1, faces, axis=1 + axis) - lax.slice_in_dim(flux, 0, faces - 1, axis=1 + axis)
        total = total - change
    return total

def drag_tile(flat, cells, slots, live):
    values = flat[cells] + WIND
    onehot = jnp.where((slots[:, None] == jnp.arange(TURB, dtype=jnp.int32)[None, :]) & (live[:, None] == 1), 1.0, 0.0).astype(jnp.float32)
    sums = jnp.dot(values, onehot, precision=HIGH)
    counts = lax.optimization_barrier(jnp.sum(onehot, axis=0))
    mean = sums / jnp.maximum(counts, 1.0)
    thrust = -0.5 * THRUST * mean * jnp.abs(mean)
    per_slot = jnp.dot(onehot, thrust, precision=HIGH)
    return jnp.zeros(flat.shape, jnp.float32).at[cells].add(per_slot)

def farm_rate(field, cells, slots, live):
    padded = jnp.pad(field, ((0, 0), (2, 2), (2, 2), (0, 0)), mode='wrap')

    def tile_rate(index):
        block = lax.dynamic_slice_in_dim(padded, index * CX, CX + 4, axis=1)
        return farm_tendency(block)
    rates = lax.map(tile_rate, jnp.arange(N_GX, dtype=jnp.int32))
    rates = jnp.moveaxis(rates, 0, 1).reshape(3, NX, NY, NZ)
    tiles = field[0].reshape(N_GX, CX, N_GY, CY, NZ).transpose(0, 2, 1, 3, 4).reshape(N_GX, N_GY, CX * CY * NZ)
    forces = jax.vmap(jax.vmap(drag_tile))(tiles, cells, slots, live)
    forces = forces.reshape(N_GX, N_GY, CX, CY, NZ).transpose(0, 2, 1, 3, 4).reshape(NX, NY, NZ)
    return rates.at[0].add(forces)

def precursor_step(field):
    component = jnp.arange(3)[:, None, None, None]
    height = jnp.arange(NZ)[None, None, None, :]
    field = jnp.where((component == 2) & (height == NZ - 1), 0.0, field)
    spec = jnp.fft.rfft(field, axis=1)[:, :NX // 2]
    spec = jnp.fft.fft(spec, axis=2)
    yindex = jnp.arange(NY)
    spec = jnp.where((yindex == NY // 2)[None, None, :, None], 0.0, spec)
    kx = 2.0 * math.pi / NX * jnp.arange(NX // 2).astype(jnp.float32)
    ky = 2.0 * math.pi / NY * jnp.where(yindex < NY // 2, yindex, yindex - NY).astype(jnp.float32)
    kx = kx[:, None, None]
    ky = ky[None, :, None]
    hor = kx * kx + ky * ky
    u_hat, v_hat, w_hat = (spec[0], spec[1], spec[2])
    below = w_hat - jnp.pad(w_hat, ((0, 0), (0, 0), (1, 0)))[:, :, :-1]
    div = 1j * kx * u_hat + 1j * ky * v_hat + below
    level = jnp.arange(NZ)
    ends = jnp.where((level == 0) | (level == NZ - 1), -1.0, -2.0).astype(jnp.float32)
    pin = jnp.where((hor == 0.0) & (level == 0)[None, None, :], -1.0, 0.0).astype(jnp.float32)
    diag = ends[None, None, :] - hor + pin
    lower = jnp.broadcast_to(jnp.where(level == 0, 0.0, 1.0).astype(jnp.float32), diag.shape)
    upper = jnp.broadcast_to(jnp.where(level == NZ - 1, 0.0, 1.0).astype(jnp.float32), diag.shape)
    rhs = jnp.stack([jnp.real(div), jnp.imag(div)], axis=-1)
    solved = lax.linalg.tridiagonal_solve(lower, diag, upper, rhs)
    press = solved[..., 0] + 1j * solved[..., 1]
    grad = jnp.pad(press, ((0, 0), (0, 0), (0, 1)))[:, :, 1:] - press
    grad = jnp.where((level == NZ - 1)[None, None, :], 0.0, grad)
    decay = jnp.exp(-DIFFUSE * hor)
    u_hat = (u_hat - 1j * kx * press) * decay
    v_hat = (v_hat - 1j * ky * press) * decay
    w_hat = (w_hat - grad) * decay
    spec = jnp.stack([u_hat, v_hat, w_hat])
    spec = jnp.fft.ifft(spec, axis=2)
    spec = jnp.pad(spec, ((0, 0), (0, 1), (0, 0), (0, 0)))
    return jnp.fft.irfft(spec, n=NX, axis=1).astype(jnp.float32)

def reference(farm_velocity, precursor_velocity, turb_cell, turb_slot, disk_mask):
    precursor_new = precursor_step(precursor_velocity)
    state = farm_velocity.at[:, :NF].set(precursor_new[:, NX - NF:])
    section_one = state + STEP * farm_rate(state, turb_cell, turb_slot, disk_mask)
    section_two = 0.75 * state + 0.25 * (section_one + STEP * farm_rate(section_one, turb_cell, turb_slot, disk_mask))
    farm_new = state / 3.0 + 2.0 / 3.0 * (section_two + STEP * farm_rate(section_two, turb_cell, turb_slot, disk_mask))
    return (farm_new, precursor_new)
```

```python
import functools
import math

import jax
import jax.numpy as jnp
import numpy as np
from jax import lax
from jax.experimental import pallas as pl
from jax.experimental.pallas import tpu as pltpu
from jax.sharding import PartitionSpec as P

NF = 48
TURB = 16
WIND = 3.0
STEP = 0.1
SMAG = 0.0289
THRUST = 1.33
DIFFUSE = 0.05
HIGH = lax.Precision.HIGHEST
MESH = pl.DeviceIdType.MESH
AXES = ("gx", "gy")


def split_pair(table):
    table = np.asarray(table, np.float32)
    head = table.astype(jnp.bfloat16)
    tail = (table - head.astype(np.float32)).astype(jnp.bfloat16)
    return np.stack([head, tail])


def spectral_tables(across, spanwise, width, depth, levels):
    count = across * spanwise
    total_x, total_y = across * width, spanwise * depth
    groups = -(-levels // count)
    order = np.arange(groups * count)[:, None]
    height = np.arange(levels)[None, :]
    inside = order < levels
    scale = np.where(order == 0, math.sqrt(1.0 / levels), math.sqrt(2.0 / levels)) * inside
    centre = scale * np.cos(math.pi / (2 * levels) * (order * (2 * height + 1) % (4 * levels)))
    face = (
        math.sqrt(2.0 / levels)
        * np.sin(math.pi / levels * (order * (height + 1) % (2 * levels)))
        * ((height < levels - 1) & (order > 0) & inside)
    )
    vertical = np.stack([split_pair(centre), split_pair(face)])
    rise = 2.0 * np.sin(np.minimum(order, levels)[:, 0] * (math.pi / (2 * levels)))
    tile = np.arange(count)
    tile_x, tile_y = tile // spanwise, tile % spanwise
    turn = 2.0 * math.pi * (np.outer(tile_x, tile_x) / across + np.outer(tile_y, tile_y) / spanwise)
    outer = np.concatenate([np.cos(turn), -np.sin(turn)], axis=0)
    outer_back = np.concatenate([np.cos(turn), -np.sin(turn)], axis=1)
    lane = np.arange(width * depth)
    lane_x, lane_y = lane // depth, lane % depth
    angle = 2.0 * math.pi * (np.outer(tile_x, lane_x) / total_x + np.outer(tile_y, lane_y) / total_y)
    twist = np.stack([np.cos(angle), -np.sin(angle)])
    turn = 2.0 * math.pi * (np.outer(lane_x, lane_x) / width + np.outer(lane_y, lane_y) / depth)
    real, imag = np.cos(turn), np.sin(turn)
    inner_forward = np.block([[real, -imag], [imag, real]])
    inner_back = np.block([[real, imag], [-imag, real]])
    k = tile_x[:, None] + across * lane_x[None, :]
    q = tile_y[:, None] + spanwise * lane_y[None, :]
    kx = 2.0 * math.pi / total_x * np.where(k < total_x // 2, k, k - total_x)
    ky = 2.0 * math.pi / total_y * np.where(q < total_y // 2, q, q - total_y)
    hor = kx * kx + ky * ky
    kept = (k != total_x // 2) & (q != total_y // 2)
    decay = np.exp(-DIFFUSE * hor) * kept / (total_x * total_y)
    waves = np.stack([kx, ky, hor, decay])
    return (
        vertical,
        split_pair(outer),
        split_pair(outer_back),
        split_pair(inner_forward),
        split_pair(inner_back),
        twist.astype(np.float32),
        waves.astype(np.float32),
        rise.astype(np.float32),
    )


def halves(value):
    head = value.astype(jnp.bfloat16)
    return head, (value - head.astype(jnp.float32)).astype(jnp.bfloat16)


def product(left, right, dims=((1,), (0,))):
    dot = functools.partial(
        lax.dot_general, dimension_numbers=(dims, ((), ())), preferred_element_type=jnp.float32
    )
    return dot(left[0], right[0]) + (dot(left[0], right[1]) + dot(left[1], right[0]))


def parts(ref):
    return ref[0], ref[1]


def exchange(position, count, spanwise, source, target, send_sem, recv_sem):
    def copy(peer, slot):
        return pltpu.make_async_remote_copy(
            src_ref=source.at[peer],
            dst_ref=target.at[slot],
            send_sem=send_sem.at[peer],
            recv_sem=recv_sem.at[slot],
            device_id=(peer // spanwise, peer % spanwise),
            device_id_type=MESH,
        )

    @pl.loop(1, count)
    def _(step):
        copy((position + step) % count, position).start()

    target[position] = source[position]

    @pl.loop(1, count)
    def _(step):
        peer = (position + step) % count
        copy(peer, peer).wait_recv()

    @pl.loop(1, count)
    def _(step):
        peer = (position + step) % count
        copy(peer, peer).wait_send()


def precursor_body(
    across, spanwise, pre, vertical, outer, outer_back, inner_f, inner_b, twist, waves, rise,
    out, send, recv, send_two, recv_two, send_sem, recv_sem,
):
    count = across * spanwise
    row, column = lax.axis_index("gx"), lax.axis_index("gy")
    position = row * spanwise + column
    comps, area, levels = pre.shape
    groups = send.shape[1] // comps
    barrier = pltpu.get_barrier_semaphore()

    @pl.loop(1, count)
    def _(step):
        peer = (position + step) % count
        pl.semaphore_signal(
            barrier, inc=1, device_id=(peer // spanwise, peer % spanwise), device_id_type=MESH
        )

    last = ((1,), (1,))
    for comp in range(comps):
        modes = product(parts(vertical.at[comp // 2]), halves(pre[comp]), last)
        for group in range(groups):
            send[:, group * comps + comp, :] = modes[group * count : (group + 1) * count]
    pl.semaphore_wait(barrier, count - 1)
    exchange(position, count, spanwise, send, recv, send_sem.at[0], recv_sem.at[0])

    table = parts(outer)
    cos, sin = twist[0], twist[1]
    rows = []
    for group in range(groups):
        for comp in range(comps):
            spun = product(table, halves(recv[:, group * comps + comp, :]))
            real, imag = spun[:count], spun[count:]
            rows.append(
                jnp.concatenate([real * cos - imag * sin, real * sin + imag * cos], axis=1)
            )
    spec = product(halves(jnp.concatenate(rows, axis=0)), parts(inner_f))
    kx, ky, hor, decay = waves[0], waves[1], waves[2], waves[3]
    rows = []
    for group in range(groups):
        lift = rise[group * count + position]
        real, imag = [], []
        for comp in range(comps):
            start = (group * comps + comp) * count
            real.append(spec[start : start + count, :area])
            imag.append(spec[start : start + count, area:])
        bound = hor + lift * lift
        inverse = jnp.where(bound > 0.0, -1.0 / jnp.where(bound > 0.0, bound, 1.0), 0.0)
        press_re = (lift * real[2] - kx * imag[0] - ky * imag[1]) * inverse
        press_im = (kx * real[0] + ky * real[1] + lift * imag[2]) * inverse
        new_re = [real[0] + kx * press_im, real[1] + ky * press_im, real[2] + lift * press_re]
        new_im = [imag[0] - kx * press_re, imag[1] - ky * press_re, imag[2] + lift * press_im]
        for comp in range(comps):
            rows.append(jnp.concatenate([new_re[comp] * decay, new_im[comp] * decay], axis=1))
    lines = product(halves(jnp.concatenate(rows, axis=0)), parts(inner_b))
    table = parts(outer_back)
    for slot in range(groups * comps):
        real = lines[slot * count : (slot + 1) * count, :area]
        imag = lines[slot * count : (slot + 1) * count, area:]
        spun = jnp.concatenate([real * cos + imag * sin, imag * cos - real * sin], axis=0)
        send_two[:, slot, :] = product(table, halves(spun))
    exchange(position, count, spanwise, send_two, recv_two, send_sem.at[1], recv_sem.at[1])
    for comp in range(comps):
        modes = jnp.concatenate(
            [recv_two[:, group * comps + comp, :] for group in range(groups)], axis=0
        )
        out[comp] = product(halves(modes.T), parts(vertical.at[comp // 2]))


def precursor(pre, across, spanwise):
    comps, width, depth, levels = pre.shape
    count = across * spanwise
    area = width * depth
    tables = spectral_tables(across, spanwise, width, depth, levels)
    slots = comps * -(-levels // count)
    vmem = pl.BlockSpec(memory_space=pltpu.VMEM)
    smem = pl.BlockSpec(memory_space=pltpu.SMEM)
    buffer = pltpu.VMEM((count, slots, area), jnp.float32)
    out = pl.pallas_call(
        functools.partial(precursor_body, across, spanwise),
        out_shape=jax.ShapeDtypeStruct((comps, area, levels), jnp.float32),
        in_specs=[vmem] * 8 + [smem],
        out_specs=vmem,
        scratch_shapes=[
            buffer,
            buffer,
            buffer,
            buffer,
            pltpu.SemaphoreType.DMA((2, count)),
            pltpu.SemaphoreType.DMA((2, count)),
        ],
        compiler_params=pltpu.CompilerParams(collective_id=0, has_side_effects=True),
        name="precursor",
    )(pre.reshape(comps, area, levels), *[jnp.asarray(table) for table in tables])
    return out.reshape(pre.shape)


def passed_along(value, axis, steps):
    count = lax.axis_size(axis)
    leading, last = (max(0, -steps), min(count, count - steps))
    return lax.ppermute(value, axis, [(source, source + steps) for source in range(leading, last)])


def extended(cells, sides, width):
    for axis, dim in sides:
        count = lax.axis_size(axis)
        head = lax.slice_in_dim(cells, 0, width, axis=dim)
        tail = lax.slice_in_dim(cells, cells.shape[dim] - width, cells.shape[dim], axis=dim)
        cells = jnp.concatenate(
            [
                lax.ppermute(tail, axis, [(i, (i + 1) % count) for i in range(count)]),
                cells,
                lax.ppermute(head, axis, [((i + 1) % count, i) for i in range(count)]),
            ],
            axis=dim,
        )
    return cells


def inner(arr, axis, start, length):
    out = arr
    for dim in range(3):
        place = out.ndim - 3 + dim
        extent = arr.shape[arr.ndim - 3 + dim]
        if dim == axis:
            out = lax.slice_in_dim(out, start, start + length, axis=place)
        else:
            out = lax.slice_in_dim(out, 1, extent - 1, axis=place)
    return out


def farm_tendency(ext):
    padded = jnp.pad(ext, ((0, 0), (0, 0), (0, 0), (2, 2)))
    cycle = padded[:, 1:-1, 1:-1, 1:-1]
    grads = []
    for axis in range(3):
        extent = padded.shape[1 + axis]
        grads.append(
            0.5 * (inner(padded, axis, 2, extent - 2) - inner(padded, axis, 0, extent - 2))
        )
    square = jnp.zeros(cycle.shape[1:], jnp.float32)
    for first in range(3):
        for second in range(3):
            strain = 0.5 * (grads[second][first] + grads[first][second])
            square = square + strain * strain
    eddy = SMAG * jnp.sqrt(2.0 * square)
    advect = cycle + jnp.array([WIND, 0.0, 0.0], jnp.float32)[:, None, None, None]
    total = jnp.zeros((3,) + tuple((n - 2 for n in cycle.shape[1:])), jnp.float32)
    for axis in range(3):
        extent = cycle.shape[1 + axis]
        low_f = inner(cycle, axis, 0, extent - 1)
        high_f = inner(cycle, axis, 1, extent - 1)
        low_v = inner(advect[axis], axis, 0, extent - 1)
        high_v = inner(advect[axis], axis, 1, extent - 1)
        low_e = inner(eddy, axis, 0, extent - 1)
        high_e = inner(eddy, axis, 1, extent - 1)
        flux = 0.25 * (low_v + high_v) * (low_f + high_f) - 0.5 * (low_e + high_e) * (
            high_f - low_f
        )
        faces = extent - 1
        change = lax.slice_in_dim(flux, 1, faces, axis=1 + axis) - lax.slice_in_dim(
            flux, 0, faces - 1, axis=1 + axis
        )
        total = total - change
    return total


def drag_tile(flat, cells, slots, live):
    values = flat[cells] + WIND
    onehot = jnp.where(
        (slots[:, None] == jnp.arange(TURB, dtype=jnp.int32)[None, :]) & (live[:, None] == 1),
        1.0,
        0.0,
    ).astype(jnp.float32)
    sums = jnp.dot(values, onehot, precision=HIGH)
    counts = jnp.sum(onehot, axis=0)
    mean = sums / jnp.maximum(counts, 1.0)
    thrust = -0.5 * THRUST * mean * jnp.abs(mean)
    per_slot = jnp.dot(onehot, thrust, precision=HIGH)
    return jnp.zeros(flat.shape, jnp.float32).at[cells].add(per_slot)


def shards(farm_velocity, precursor_velocity, turb_cell, turb_slot, disk_mask):
    across = lax.axis_size("gx")
    spanwise = lax.axis_size("gy")
    row = lax.axis_index("gx")
    comps, width, depth, levels = precursor_velocity.shape
    physical = precursor(precursor_velocity, across, spanwise)
    incoming = passed_along(physical, "gx", NF // width - across)
    position = row * width + jnp.arange(width, dtype=jnp.int32)[None, :, None, None]
    state = jnp.where(position < NF, incoming, farm_velocity)
    cells = turb_cell.reshape(-1)
    slots = turb_slot.reshape(-1)
    live = disk_mask.reshape(-1)

    def rate_of(current):
        ext = extended(current, (("gx", 1), ("gy", 2)), 2)
        tendency = farm_tendency(ext)
        force = drag_tile(current[0].reshape(-1), cells, slots, live).reshape(current.shape[1:])
        return tendency.at[0].add(force)

    section_one = state + STEP * rate_of(state)
    section_two = 0.75 * state + 0.25 * (section_one + STEP * rate_of(section_one))
    farm_new = state / 3.0 + 2.0 / 3.0 * (section_two + STEP * rate_of(section_two))
    return (farm_new, physical)


def solution(mesh):
    return jax.shard_map(
        shards,
        mesh=mesh,
        in_specs=(
            P(None, "gx", "gy", None),
            P(None, "gx", "gy", None),
            P("gx", "gy", None),
            P("gx", "gy", None),
            P("gx", "gy", None),
        ),
        out_specs=(P(None, "gx", "gy", None), P(None, "gx", "gy", None)),
        check_vma=False,
    )
```

```python
import functools
import math

import jax
import jax.numpy as jnp
import numpy as np
from jax import lax
from jax.experimental import pallas as pl
from jax.experimental.pallas import tpu as pltpu
from jax.sharding import PartitionSpec as P

NF = 48
TURB = 16
WIND = 3.0
STEP = 0.1
SMAG = 0.0289
THRUST = 1.33
DIFFUSE = 0.05
HIGH = lax.Precision.HIGHEST
MESH = pl.DeviceIdType.MESH
AXES = ("gx", "gy")


def split_pair(table):
    table = np.asarray(table, np.float32)
    head = table.astype(jnp.bfloat16)
    tail = (table - head.astype(np.float32)).astype(jnp.bfloat16)
    return np.stack([head, tail])


def spectral_tables(across, spanwise, width, depth, levels, lanes):
    count = across * spanwise
    total_x, total_y = across * width, spanwise * depth
    groups = -(-levels // count)
    order = np.arange(groups * count)[:, None]
    height = np.arange(levels)[None, :]
    inside = order < levels
    scale = np.where(order == 0, math.sqrt(1.0 / levels), math.sqrt(2.0 / levels)) * inside
    centre = scale * np.cos(math.pi / (2 * levels) * (order * (2 * height + 1) % (4 * levels)))
    face = (
        math.sqrt(2.0 / levels)
        * np.sin(math.pi / levels * (order * (height + 1) % (2 * levels)))
        * ((height < levels - 1) & (order > 0) & inside)
    )
    beyond = ((0, 0), (0, lanes - levels))
    vertical = np.stack([split_pair(np.pad(table, beyond)) for table in (centre, face)])
    rise = 2.0 * np.sin(np.minimum(order, levels)[:, 0] * (math.pi / (2 * levels)))
    tile = np.arange(count)
    tile_x, tile_y = tile // spanwise, tile % spanwise
    turn = 2.0 * math.pi * (np.outer(tile_x, tile_x) / across + np.outer(tile_y, tile_y) / spanwise)
    outer = np.concatenate([np.cos(turn), -np.sin(turn)], axis=0)
    outer_back = np.concatenate([np.cos(turn), -np.sin(turn)], axis=1)
    lane = np.arange(width * depth)
    lane_x, lane_y = lane // depth, lane % depth
    angle = 2.0 * math.pi * (np.outer(tile_x, lane_x) / total_x + np.outer(tile_y, lane_y) / total_y)
    twist = np.stack([np.cos(angle), -np.sin(angle)])
    turn = 2.0 * math.pi * (np.outer(lane_x, lane_x) / width + np.outer(lane_y, lane_y) / depth)
    real, imag = np.cos(turn), np.sin(turn)
    inner_forward = np.block([[real, -imag], [imag, real]])
    inner_back = np.block([[real, imag], [-imag, real]])
    k = tile_x[:, None] + across * lane_x[None, :]
    q = tile_y[:, None] + spanwise * lane_y[None, :]
    kx = 2.0 * math.pi / total_x * np.where(k < total_x // 2, k, k - total_x)
    ky = 2.0 * math.pi / total_y * np.where(q < total_y // 2, q, q - total_y)
    hor = kx * kx + ky * ky
    kept = (k != total_x // 2) & (q != total_y // 2)
    decay = np.exp(-DIFFUSE * hor) * kept / (total_x * total_y)
    waves = np.stack([kx, ky, hor, decay])
    return (
        vertical,
        split_pair(outer),
        split_pair(outer_back),
        split_pair(inner_forward),
        split_pair(inner_back),
        twist.astype(np.float32),
        waves.astype(np.float32),
        rise.astype(np.float32),
    )


def halves(value):
    head = value.astype(jnp.bfloat16)
    return head, (value - head.astype(jnp.float32)).astype(jnp.bfloat16)


def product(left, right, dims=((1,), (0,))):
    dot = functools.partial(
        lax.dot_general, dimension_numbers=(dims, ((), ())), preferred_element_type=jnp.float32
    )
    return dot(left[0], right[0]) + (dot(left[0], right[1]) + dot(left[1], right[0]))


def parts(ref):
    return ref[0], ref[1]


def exchange(position, count, spanwise, source, target, send_sem, recv_sem):
    def copy(peer, slot):
        return pltpu.make_async_remote_copy(
            src_ref=source.at[peer],
            dst_ref=target.at[slot],
            send_sem=send_sem.at[peer],
            recv_sem=recv_sem.at[slot],
            device_id=(peer // spanwise, peer % spanwise),
            device_id_type=MESH,
        )

    @pl.loop(1, count)
    def _(step):
        copy((position + step) % count, position).start()

    target[position] = source[position]

    @pl.loop(1, count)
    def _(step):
        peer = (position + step) % count
        copy(peer, peer).wait_recv()

    @pl.loop(1, count)
    def _(step):
        peer = (position + step) % count
        copy(peer, peer).wait_send()


WEIGHTS = ((0.0, 1.0), (0.75, 0.25), (1.0 / 3.0, 2.0 / 3.0))
SIDES = ((-1, 0), (1, 0), (0, -1), (0, 1), (-1, -1), (-1, 1), (1, -1), (1, 1))


def halo_copies(row, column, across, spanwise, section, field, edge, edge_in, halo_sem):
    width = field.shape[2] - 4
    depth = field.shape[3] // 2
    copies = []
    for number, (dx, dy) in enumerate(SIDES):
        first = {-1: 0, 0: 0, 1: width - 2}[dx]
        extent = width if dx == 0 else 2
        landing = {-1: width + 2, 0: 2, 1: 0}[dx]
        if dy == 0:
            source = field.at[section, :, pl.ds(first + 2, extent), pl.ds(0, depth), :]
            target = field.at[section, :, pl.ds(landing, extent), pl.ds(0, depth), :]
        else:
            source = edge.at[section, (dy + 1) // 2, :, pl.ds(first, extent)]
            target = edge_in.at[section, (1 - dy) // 2, :, pl.ds(landing, extent)]
        copies.append(
            pltpu.make_async_remote_copy(
                src_ref=source,
                dst_ref=target,
                send_sem=halo_sem.at[0, section, number],
                recv_sem=halo_sem.at[1, section, number],
                device_id=((row + dx + across) % across, (column + dy + spanwise) % spanwise),
                device_id_type=MESH,
            )
        )
    return copies


def turbine_tables(levels, cell, slot, live, one_row, one_level, one_turb):
    cells = cell[...]
    area, slots = one_row.shape
    begin = levels * lax.broadcasted_iota(jnp.int32, (area, slots), 0)
    reached = cells >= begin
    one_row[...] = jnp.where(reached & (cells < begin + levels), 1.0, 0.0).astype(jnp.bfloat16)
    passed_rows = jnp.sum(jnp.where(reached, 1, 0), axis=0, keepdims=True) - 1
    level = cells - levels * passed_rows
    one_level[...] = jnp.where(
        lax.broadcasted_iota(jnp.int32, one_level.shape, 0) == level, 1.0, 0.0
    )
    one_turb[...] = jnp.where(
        (lax.broadcasted_iota(jnp.int32, one_turb.shape, 0) == slot[...]) & (live[...] == 1),
        1.0,
        0.0,
    )


def drag_force(flow, one_row, one_level, one_turb, force):
    rows = one_row[...]
    head, tail = halves(flow.T)
    dot = functools.partial(jnp.dot, preferred_element_type=jnp.float32)
    columns = dot(head, rows) + dot(tail, rows)
    values = jnp.sum(columns * one_level[...], axis=0, keepdims=True) + WIND
    turbines = one_turb[...]
    sums = jnp.sum(turbines * values, axis=1, keepdims=True)
    counts = jnp.sum(turbines, axis=1, keepdims=True)
    mean = sums / jnp.maximum(counts, 1.0)
    thrust = -0.5 * THRUST * mean * jnp.abs(mean)
    per_slot = jnp.sum(turbines * thrust, axis=0, keepdims=True)
    head, tail = halves(one_level[...] * per_slot)
    dot = functools.partial(
        lax.dot_general,
        dimension_numbers=(((1,), (1,)), ((), ())),
        preferred_element_type=jnp.float32,
    )
    force[...] = (dot(rows, head) + dot(rows, tail)).reshape(force.shape)


def rate_section(levels, now, start, eddy, force, weight, fresh_weight, target, final):
    comps, planes, rows, lanes = now.shape
    width, depth = planes - 4, rows // 2

    @pl.loop(0, width + 2)
    def _(plane):
        centre = [now[comp, plane + 1] for comp in range(comps)]
        diff = []
        for comp in range(comps):
            value = centre[comp]
            diff.append(
                (
                    now[comp, plane + 2] - now[comp, plane],
                    pltpu.roll(value, rows - 1, 0) - pltpu.roll(value, 1, 0),
                    pltpu.roll(value, lanes - 1, 1) - pltpu.roll(value, 1, 1),
                )
            )
        cross = [diff[a][b] + diff[b][a] for a, b in ((0, 1), (0, 2), (1, 2))]
        square = sum(diff[a][a] * diff[a][a] for a in range(3)) + 0.5 * sum(
            value * value for value in cross
        )
        eddy[plane] = SMAG * jnp.sqrt(0.5 * square)

    def flux(carrier, carrier_next, value, value_next, mixing):
        return 0.25 * (carrier + carrier_next) * (value + value_next) - mixing * (
            value_next - value
        )

    def x_flux(plane):
        low = [now[comp, plane + 1, :depth] for comp in range(comps)]
        high = [now[comp, plane + 2, :depth] for comp in range(comps)]
        mixing = 0.5 * (eddy[plane, :depth] + eddy[plane + 1, :depth])
        return tuple(
            flux(low[0] + WIND, high[0] + WIND, low[comp], high[comp], mixing)
            for comp in range(comps)
        )

    def one_plane(plane, below):
        above = x_flux(plane + 1)
        whole = [now[comp, plane + 2] for comp in range(comps)]
        whole_eddy = eddy[plane + 1]
        side = [pltpu.roll(value, rows - 1, 0) for value in whole]
        mixing = 0.5 * (whole_eddy + pltpu.roll(whole_eddy, rows - 1, 0))
        span = [flux(whole[1], side[1], whole[comp], side[comp], mixing) for comp in range(comps)]
        own = [value[:depth] for value in whole]
        own_eddy = whole_eddy[:depth]
        over = [pltpu.roll(value, lanes - 1, 1) for value in own]
        mixing = 0.5 * (own_eddy + pltpu.roll(own_eddy, lanes - 1, 1))
        inside = lax.broadcasted_iota(jnp.int32, (depth, lanes), 1) < levels
        for comp in range(comps):
            rise = flux(own[2], over[2], own[comp], over[comp], mixing)
            rate = (
                (below[comp] - above[comp])
                + (pltpu.roll(span[comp], 1, 0) - span[comp])[:depth]
                + (pltpu.roll(rise, 1, 1) - rise)
            )
            if comp == 0:
                rate = rate + force[plane]
            fresh = fresh_weight * (own[comp] + STEP * rate)
            if weight:
                fresh = fresh + weight * start[comp, plane + 2, :depth]
            if final:
                target[comp, pl.ds(pl.multiple_of(plane * depth, depth), depth), :] = fresh[
                    :, :levels
                ]
            else:
                target[comp, plane + 2, :depth] = jnp.where(inside, fresh, 0.0)
        return above

    lax.fori_loop(0, width, one_plane, x_flux(0))


def step_body(
    across, spanwise, farm, pre, cell, slot, live, vertical, outer, outer_back, inner_f, inner_b,
    twist, waves, rise, farm_out, out, send, recv, send_two, recv_two, field, eddy, force, edge,
    edge_in, passed, one_row, one_level, one_turb, send_sem, recv_sem, pass_sem, halo_sem,
):
    count = across * spanwise
    row, column = lax.axis_index("gx"), lax.axis_index("gy")
    position = row * spanwise + column
    comps, area, levels = pre.shape
    lanes = field.shape[-1]
    depth = field.shape[-2] // 2
    width = area // depth
    field[...] = jnp.zeros_like(field)
    groups = send.shape[1] // comps
    barrier = pltpu.get_barrier_semaphore()

    @pl.loop(1, count)
    def _(step):
        peer = (position + step) % count
        pl.semaphore_signal(
            barrier, inc=1, device_id=(peer // spanwise, peer % spanwise), device_id_type=MESH
        )

    last = ((1,), (1,))
    for comp in range(comps):
        modes = product((vertical[comp // 2, 0][:, :levels], vertical[comp // 2, 1][:, :levels]), halves(pre[comp]), last)
        for group in range(groups):
            send[:, group * comps + comp, :] = modes[group * count : (group + 1) * count]
    pl.semaphore_wait(barrier, count - 1)
    exchange(position, count, spanwise, send, recv, send_sem.at[0], recv_sem.at[0])
    turbine_tables(levels, cell, slot, live, one_row, one_level, one_turb)

    table = parts(outer)
    cos, sin = twist[0], twist[1]
    rows = []
    for group in range(groups):
        for comp in range(comps):
            spun = product(table, halves(recv[:, group * comps + comp, :]))
            real, imag = spun[:count], spun[count:]
            rows.append(
                jnp.concatenate([real * cos - imag * sin, real * sin + imag * cos], axis=1)
            )
    spec = product(halves(jnp.concatenate(rows, axis=0)), parts(inner_f))
    kx, ky, hor, decay = waves[0], waves[1], waves[2], waves[3]
    rows = []
    for group in range(groups):
        lift = rise[group * count + position]
        real, imag = [], []
        for comp in range(comps):
            start = (group * comps + comp) * count
            real.append(spec[start : start + count, :area])
            imag.append(spec[start : start + count, area:])
        bound = hor + lift * lift
        inverse = jnp.where(bound > 0.0, -1.0 / jnp.where(bound > 0.0, bound, 1.0), 0.0)
        press_re = (lift * real[2] - kx * imag[0] - ky * imag[1]) * inverse
        press_im = (kx * real[0] + ky * real[1] + lift * imag[2]) * inverse
        new_re = [real[0] + kx * press_im, real[1] + ky * press_im, real[2] + lift * press_re]
        new_im = [imag[0] - kx * press_re, imag[1] - ky * press_re, imag[2] + lift * press_im]
        for comp in range(comps):
            rows.append(jnp.concatenate([new_re[comp] * decay, new_im[comp] * decay], axis=1))
    lines = product(halves(jnp.concatenate(rows, axis=0)), parts(inner_b))
    table = parts(outer_back)
    for slot in range(groups * comps):
        real = lines[slot * count : (slot + 1) * count, :area]
        imag = lines[slot * count : (slot + 1) * count, area:]
        spun = jnp.concatenate([real * cos + imag * sin, imag * cos - real * sin], axis=0)
        send_two[:, slot, :] = product(table, halves(spun))
    exchange(position, count, spanwise, send_two, recv_two, send_sem.at[1], recv_sem.at[1])
    fringes = NF // width
    shift = across - fringes

    def fringe(comp):
        return pltpu.make_async_remote_copy(
            src_ref=passed.at[comp],
            dst_ref=field.at[0, comp, pl.ds(2, width), pl.ds(0, depth), :],
            send_sem=pass_sem.at[0, comp],
            recv_sem=pass_sem.at[1, comp],
            device_id=((row + across - shift) % across, column),
            device_id_type=MESH,
        )

    for comp in range(comps):
        modes = jnp.concatenate(
            [recv_two[:, group * comps + comp, :] for group in range(groups)], axis=0
        )
        fresh = product(halves(modes.T), parts(vertical.at[comp // 2]))
        out[comp] = fresh[:, :levels]
        passed[comp] = fresh.reshape(width, depth, lanes)

        @pl.when(row >= shift)
        def _():
            fringe(comp).start()

    @pl.when(row >= fringes)
    def _():
        for comp in range(comps):
            field[0, comp, 2 : width + 2, :depth, :levels] = farm[comp].reshape(
                width, depth, levels
            )

    @pl.when(row < fringes)
    def _():
        for comp in range(comps):
            fringe(comp).wait_recv()

    for section, (weight, fresh_weight) in enumerate(WEIGHTS):
        for side, start in ((0, 0), (1, depth - 2)):
            edge[section, side] = field[section, :, 2 : width + 2, start : start + 2, :]
        copies = halo_copies(
            row, column, across, spanwise, section, field, edge, edge_in, halo_sem
        )
        for copy in copies:
            copy.start()
        drag_force(
            field[section, 0, 2 : width + 2, :depth, :].reshape(area, lanes),
            one_row, one_level, one_turb, force,
        )
        for copy in copies:
            copy.wait_recv()
        for comp in range(comps):
            field[section, comp, :, depth : depth + 2, :] = edge_in[section, 1, comp]
            field[section, comp, :, 2 * depth - 2 :, :] = edge_in[section, 0, comp]
        final = section == len(WEIGHTS) - 1
        rate_section(
            levels, field.at[section], field.at[0], eddy, force, weight, fresh_weight,
            farm_out if final else field.at[section + 1], final,
        )
        for copy in copies:
            copy.wait_send()

    @pl.when(row >= shift)
    def _():
        for comp in range(comps):
            fringe(comp).wait_send()


def shards(farm_velocity, precursor_velocity, turb_cell, turb_slot, disk_mask):
    across = lax.axis_size("gx")
    spanwise = lax.axis_size("gy")
    comps, width, depth, levels = precursor_velocity.shape
    count = across * spanwise
    area = width * depth
    lanes = -(-(levels + 2) // 128) * 128
    slots = turb_cell.shape[-1]
    tables = spectral_tables(across, spanwise, width, depth, levels, lanes)
    messages = comps * -(-levels // count)
    sections = len(WEIGHTS)
    vmem = pl.BlockSpec(memory_space=pltpu.VMEM)
    smem = pl.BlockSpec(memory_space=pltpu.SMEM)
    buffer = pltpu.VMEM((count, messages, area), jnp.float32)
    edges = pltpu.VMEM((sections, 2, comps, width, 2, lanes), jnp.float32)
    edges_in = pltpu.VMEM((sections, 2, comps, width + 4, 2, lanes), jnp.float32)
    field = jax.ShapeDtypeStruct((comps, area, levels), jnp.float32)
    farm_new, fresh = pl.pallas_call(
        functools.partial(step_body, across, spanwise),
        out_shape=(field, field),
        in_specs=[vmem] * 12 + [smem],
        out_specs=(vmem, vmem),
        scratch_shapes=[
            buffer,
            buffer,
            buffer,
            buffer,
            pltpu.VMEM((sections, comps, width + 4, 2 * depth, lanes), jnp.float32),
            pltpu.VMEM((width + 2, 2 * depth, lanes), jnp.float32),
            pltpu.VMEM((width, depth, lanes), jnp.float32),
            edges,
            edges_in,
            pltpu.VMEM((comps, width, depth, lanes), jnp.float32),
            pltpu.VMEM((area, slots), jnp.bfloat16),
            pltpu.VMEM((lanes, slots), jnp.float32),
            pltpu.VMEM((TURB, slots), jnp.float32),
            pltpu.SemaphoreType.DMA((2, count)),
            pltpu.SemaphoreType.DMA((2, count)),
            pltpu.SemaphoreType.DMA((2, comps)),
            pltpu.SemaphoreType.DMA((2, sections, len(SIDES))),
        ],
        compiler_params=pltpu.CompilerParams(collective_id=0, has_side_effects=True),
        name="farm_step",
    )(
        farm_velocity.reshape(field.shape),
        precursor_velocity.reshape(field.shape),
        turb_cell.reshape(1, slots),
        turb_slot.reshape(1, slots),
        disk_mask.reshape(1, slots),
        *[jnp.asarray(table) for table in tables],
    )
    return (farm_new.reshape(farm_velocity.shape), fresh.reshape(farm_velocity.shape))


def solution(mesh):
    return jax.shard_map(
        shards,
        mesh=mesh,
        in_specs=(
            P(None, "gx", "gy", None),
            P(None, "gx", "gy", None),
            P("gx", "gy", None),
            P("gx", "gy", None),
            P("gx", "gy", None),
        ),
        out_specs=(P(None, "gx", "gy", None), P(None, "gx", "gy", None)),
        check_vma=False,
    )
```

```python
import functools
import math

import jax
import jax.numpy as jnp
import numpy as np
from jax import lax
from jax.experimental import pallas as pl
from jax.experimental.pallas import tpu as pltpu
from jax.sharding import PartitionSpec as P

NF = 48
TURB = 16
WIND = 3.0
STEP = 0.1
SMAG = 0.0289
THRUST = 1.33
DIFFUSE = 0.05
HIGH = lax.Precision.HIGHEST
MESH = pl.DeviceIdType.MESH
AXES = ("gx", "gy")


def split_pair(table):
    table = np.asarray(table, np.float32)
    head = table.astype(jnp.bfloat16)
    tail = (table - head.astype(np.float32)).astype(jnp.bfloat16)
    return np.stack([head, tail])


def spectral_tables(across, spanwise, width, depth, levels, lanes):
    count = across * spanwise
    total_x, total_y = across * width, spanwise * depth
    groups = -(-levels // count)
    order = np.arange(groups * count)[:, None]
    height = np.arange(levels)[None, :]
    inside = order < levels
    scale = np.where(order == 0, math.sqrt(1.0 / levels), math.sqrt(2.0 / levels)) * inside
    centre = scale * np.cos(math.pi / (2 * levels) * (order * (2 * height + 1) % (4 * levels)))
    face = (
        math.sqrt(2.0 / levels)
        * np.sin(math.pi / levels * (order * (height + 1) % (2 * levels)))
        * ((height < levels - 1) & (order > 0) & inside)
    )
    beyond = ((0, 0), (0, lanes - levels))
    vertical = np.stack([split_pair(np.pad(table, beyond)) for table in (centre, face)])
    rise = 2.0 * np.sin(np.minimum(order, levels)[:, 0] * (math.pi / (2 * levels)))
    tile = np.arange(count)
    tile_x, tile_y = tile // spanwise, tile % spanwise
    turn = 2.0 * math.pi * (np.outer(tile_x, tile_x) / across + np.outer(tile_y, tile_y) / spanwise)
    outer = np.concatenate([np.cos(turn), -np.sin(turn)], axis=0)
    outer_back = np.concatenate([np.cos(turn), -np.sin(turn)], axis=1)
    lane = np.arange(width * depth)
    lane_x, lane_y = lane // depth, lane % depth
    angle = 2.0 * math.pi * (np.outer(tile_x, lane_x) / total_x + np.outer(tile_y, lane_y) / total_y)
    twist = np.stack([np.cos(angle), -np.sin(angle)])
    turn = 2.0 * math.pi * (np.outer(lane_x, lane_x) / width + np.outer(lane_y, lane_y) / depth)
    real, imag = np.cos(turn), np.sin(turn)
    inner_forward = np.block([[real, -imag], [imag, real]])
    inner_back = np.block([[real, imag], [-imag, real]])
    k = tile_x[:, None] + across * lane_x[None, :]
    q = tile_y[:, None] + spanwise * lane_y[None, :]
    kx = 2.0 * math.pi / total_x * np.where(k < total_x // 2, k, k - total_x)
    ky = 2.0 * math.pi / total_y * np.where(q < total_y // 2, q, q - total_y)
    hor = kx * kx + ky * ky
    kept = (k != total_x // 2) & (q != total_y // 2)
    decay = np.exp(-DIFFUSE * hor) * kept / (total_x * total_y)
    waves = np.stack([kx, ky, hor, decay])
    return (
        vertical,
        split_pair(outer),
        split_pair(outer_back),
        split_pair(inner_forward),
        split_pair(inner_back),
        twist.astype(np.float32),
        waves.astype(np.float32),
        rise.astype(np.float32),
    )


def halves(value):
    head = value.astype(jnp.bfloat16)
    return head, (value - head.astype(jnp.float32)).astype(jnp.bfloat16)


def product(left, right, dims=((1,), (0,))):
    dot = functools.partial(
        lax.dot_general, dimension_numbers=(dims, ((), ())), preferred_element_type=jnp.float32
    )
    return dot(left[0], right[0]) + (dot(left[0], right[1]) + dot(left[1], right[0]))


def parts(ref):
    return ref[0], ref[1]


def exchange(position, count, spanwise, source, target, send_sem, recv_sem):
    def copy(peer, slot):
        return pltpu.make_async_remote_copy(
            src_ref=source.at[peer],
            dst_ref=target.at[slot],
            send_sem=send_sem.at[peer],
            recv_sem=recv_sem.at[slot],
            device_id=(peer // spanwise, peer % spanwise),
            device_id_type=MESH,
        )

    @pl.loop(1, count)
    def _(step):
        copy((position + step) % count, position).start()

    target[position] = source[position]

    @pl.loop(1, count)
    def _(step):
        peer = (position + step) % count
        copy(peer, peer).wait_recv()

    @pl.loop(1, count)
    def _(step):
        peer = (position + step) % count
        copy(peer, peer).wait_send()


WEIGHTS = ((0.0, 1.0), (0.75, 0.25), (1.0 / 3.0, 2.0 / 3.0))
SIDES = ((0, -1), (0, 1), (-1, -1), (-1, 1), (1, -1), (1, 1), (-1, 0), (1, 0))


def halo_copies(row, column, across, spanwise, section, field, edge, edge_in, halo_sem):
    width = field.shape[2] - 4
    depth = field.shape[3] // 2
    copies = []
    for number, (dx, dy) in enumerate(SIDES):
        first = {-1: 0, 0: 0, 1: width - 2}[dx]
        extent = width if dx == 0 else 2
        landing = {-1: width + 2, 0: 2, 1: 0}[dx]
        if dy == 0:
            source = field.at[section, :, pl.ds(first + 2, extent), pl.ds(0, depth), :]
            target = field.at[section, :, pl.ds(landing, extent), pl.ds(0, depth), :]
        else:
            source = edge.at[section, (dy + 1) // 2, :, pl.ds(first, extent)]
            target = edge_in.at[section, (1 - dy) // 2, :, pl.ds(landing, extent)]
        copies.append(
            pltpu.make_async_remote_copy(
                src_ref=source,
                dst_ref=target,
                send_sem=halo_sem.at[0, section, number],
                recv_sem=halo_sem.at[1, section, number],
                device_id=((row + dx + across) % across, (column + dy + spanwise) % spanwise),
                device_id_type=MESH,
            )
        )
    return copies


def turbine_tables(levels, cell, slot, live, one_row, one_level, one_turb):
    cells = cell[...]
    area, slots = one_row.shape
    begin = levels * lax.broadcasted_iota(jnp.int32, (area, slots), 0)
    reached = cells >= begin
    one_row[...] = jnp.where(reached & (cells < begin + levels), 1.0, 0.0).astype(jnp.bfloat16)
    passed_rows = jnp.sum(jnp.where(reached, 1, 0), axis=0, keepdims=True) - 1
    level = cells - levels * passed_rows
    one_level[...] = jnp.where(
        lax.broadcasted_iota(jnp.int32, one_level.shape, 0) == level, 1.0, 0.0
    )
    one_turb[...] = jnp.where(
        (lax.broadcasted_iota(jnp.int32, one_turb.shape, 0) == slot[...]) & (live[...] == 1),
        1.0,
        0.0,
    )


def drag_force(flow, one_row, one_level, one_turb, force):
    rows = one_row[...]
    head, tail = halves(flow.T)
    dot = functools.partial(jnp.dot, preferred_element_type=jnp.float32)
    columns = dot(head, rows) + dot(tail, rows)
    values = jnp.sum(columns * one_level[...], axis=0, keepdims=True) + WIND
    turbines = one_turb[...]
    sums = jnp.sum(turbines * values, axis=1, keepdims=True)
    counts = jnp.sum(turbines, axis=1, keepdims=True)
    mean = sums / jnp.maximum(counts, 1.0)
    thrust = -0.5 * THRUST * mean * jnp.abs(mean)
    per_slot = jnp.sum(turbines * thrust, axis=0, keepdims=True)
    head, tail = halves(one_level[...] * per_slot)
    dot = functools.partial(
        lax.dot_general,
        dimension_numbers=(((1,), (1,)), ((), ())),
        preferred_element_type=jnp.float32,
    )
    force[...] = (dot(rows, head) + dot(rows, tail)).reshape(force.shape)


def rate_section(levels, now, start, eddy, force, weight, fresh_weight, target, final, rest):
    comps, planes, rows, lanes = now.shape
    width, depth = planes - 4, rows // 2

    def eddy_plane(plane):
        centre = [now[comp, plane + 1] for comp in range(comps)]
        diff = []
        for comp in range(comps):
            value = centre[comp]
            diff.append(
                (
                    now[comp, plane + 2] - now[comp, plane],
                    pltpu.roll(value, rows - 1, 0) - pltpu.roll(value, 1, 0),
                    pltpu.roll(value, lanes - 1, 1) - pltpu.roll(value, 1, 1),
                )
            )
        cross = [diff[a][b] + diff[b][a] for a, b in ((0, 1), (0, 2), (1, 2))]
        square = sum(diff[a][a] * diff[a][a] for a in range(3)) + 0.5 * sum(
            value * value for value in cross
        )
        eddy[plane] = SMAG * jnp.sqrt(0.5 * square)

    def flux(carrier, carrier_next, value, value_next, mixing):
        return 0.25 * (carrier + carrier_next) * (value + value_next) - mixing * (
            value_next - value
        )

    def x_flux(plane):
        low = [now[comp, plane + 1, :depth] for comp in range(comps)]
        high = [now[comp, plane + 2, :depth] for comp in range(comps)]
        mixing = 0.5 * (eddy[plane, :depth] + eddy[plane + 1, :depth])
        return tuple(
            flux(low[0] + WIND, high[0] + WIND, low[comp], high[comp], mixing)
            for comp in range(comps)
        )

    def one_plane(plane, below):
        above = x_flux(plane + 1)
        whole = [now[comp, plane + 2] for comp in range(comps)]
        whole_eddy = eddy[plane + 1]
        side = [pltpu.roll(value, rows - 1, 0) for value in whole]
        mixing = 0.5 * (whole_eddy + pltpu.roll(whole_eddy, rows - 1, 0))
        span = [flux(whole[1], side[1], whole[comp], side[comp], mixing) for comp in range(comps)]
        own = [value[:depth] for value in whole]
        own_eddy = whole_eddy[:depth]
        over = [pltpu.roll(value, lanes - 1, 1) for value in own]
        mixing = 0.5 * (own_eddy + pltpu.roll(own_eddy, lanes - 1, 1))
        inside = lax.broadcasted_iota(jnp.int32, (depth, lanes), 1) < levels
        for comp in range(comps):
            rise = flux(own[2], over[2], own[comp], over[comp], mixing)
            rate = (
                (below[comp] - above[comp])
                + (pltpu.roll(span[comp], 1, 0) - span[comp])[:depth]
                + (pltpu.roll(rise, 1, 1) - rise)
            )
            if comp == 0:
                rate = rate + force[plane]
            fresh = fresh_weight * (own[comp] + STEP * rate)
            if weight:
                fresh = fresh + weight * start[comp, plane + 2, :depth]
            if final:
                target[comp, pl.ds(pl.multiple_of(plane * depth, depth), depth), :] = fresh[
                    :, :levels
                ]
            else:
                target[comp, plane + 2, :depth] = jnp.where(inside, fresh, 0.0)
        return above

    @pl.loop(2, width, unroll=2)
    def _(plane):
        eddy_plane(plane)

    lax.fori_loop(2, width - 2, one_plane, x_flux(2), unroll=2)
    rest()

    @pl.loop(0, 4, unroll=2)
    def _(step):
        eddy_plane(step + (step // 2) * (width - 2))

    @pl.loop(0, 2)
    def _(step):
        first = step * (width - 2)
        below = one_plane(first, x_flux(first))
        one_plane(first + 1, below)


def step_body(
    across, spanwise, farm, pre, cell, slot, live, vertical, outer, outer_back, inner_f, inner_b,
    twist, waves, rise, farm_out, out, send, recv, send_two, recv_two, field, eddy, force, edge,
    edge_in, passed, one_row, one_level, one_turb, send_sem, recv_sem, pass_sem, halo_sem,
):
    count = across * spanwise
    row, column = lax.axis_index("gx"), lax.axis_index("gy")
    position = row * spanwise + column
    comps, area, levels = pre.shape
    lanes = field.shape[-1]
    depth = field.shape[-2] // 2
    width = area // depth
    field[...] = jnp.zeros_like(field)
    groups = send.shape[1] // comps
    barrier = pltpu.get_barrier_semaphore()

    @pl.loop(1, count)
    def _(step):
        peer = (position + step) % count
        pl.semaphore_signal(
            barrier, inc=1, device_id=(peer // spanwise, peer % spanwise), device_id_type=MESH
        )

    last = ((1,), (1,))
    for comp in range(comps):
        modes = product((vertical[comp // 2, 0][:, :levels], vertical[comp // 2, 1][:, :levels]), halves(pre[comp]), last)
        for group in range(groups):
            send[:, group * comps + comp, :] = modes[group * count : (group + 1) * count]
    pl.semaphore_wait(barrier, count - 1)
    exchange(position, count, spanwise, send, recv, send_sem.at[0], recv_sem.at[0])
    turbine_tables(levels, cell, slot, live, one_row, one_level, one_turb)

    table = parts(outer)
    cos, sin = twist[0], twist[1]
    rows = []
    for group in range(groups):
        for comp in range(comps):
            spun = product(table, halves(recv[:, group * comps + comp, :]))
            real, imag = spun[:count], spun[count:]
            rows.append(
                jnp.concatenate([real * cos - imag * sin, real * sin + imag * cos], axis=1)
            )
    spec = product(halves(jnp.concatenate(rows, axis=0)), parts(inner_f))
    kx, ky, hor, decay = waves[0], waves[1], waves[2], waves[3]
    rows = []
    for group in range(groups):
        lift = rise[group * count + position]
        real, imag = [], []
        for comp in range(comps):
            start = (group * comps + comp) * count
            real.append(spec[start : start + count, :area])
            imag.append(spec[start : start + count, area:])
        bound = hor + lift * lift
        inverse = jnp.where(bound > 0.0, -1.0 / jnp.where(bound > 0.0, bound, 1.0), 0.0)
        press_re = (lift * real[2] - kx * imag[0] - ky * imag[1]) * inverse
        press_im = (kx * real[0] + ky * real[1] + lift * imag[2]) * inverse
        new_re = [real[0] + kx * press_im, real[1] + ky * press_im, real[2] + lift * press_re]
        new_im = [imag[0] - kx * press_re, imag[1] - ky * press_re, imag[2] + lift * press_im]
        for comp in range(comps):
            rows.append(jnp.concatenate([new_re[comp] * decay, new_im[comp] * decay], axis=1))
    lines = product(halves(jnp.concatenate(rows, axis=0)), parts(inner_b))
    table = parts(outer_back)
    for slot in range(groups * comps):
        real = lines[slot * count : (slot + 1) * count, :area]
        imag = lines[slot * count : (slot + 1) * count, area:]
        spun = jnp.concatenate([real * cos + imag * sin, imag * cos - real * sin], axis=0)
        send_two[:, slot, :] = product(table, halves(spun))
    exchange(position, count, spanwise, send_two, recv_two, send_sem.at[1], recv_sem.at[1])
    fringes = NF // width
    shift = across - fringes

    def fringe(comp):
        return pltpu.make_async_remote_copy(
            src_ref=passed.at[comp],
            dst_ref=field.at[0, comp, pl.ds(2, width), pl.ds(0, depth), :],
            send_sem=pass_sem.at[0, comp],
            recv_sem=pass_sem.at[1, comp],
            device_id=((row + across - shift) % across, column),
            device_id_type=MESH,
        )

    for comp in range(comps):
        modes = jnp.concatenate(
            [recv_two[:, group * comps + comp, :] for group in range(groups)], axis=0
        )
        fresh = product(halves(modes.T), parts(vertical.at[comp // 2]))
        out[comp] = fresh[:, :levels]
        passed[comp] = fresh.reshape(width, depth, lanes)

        @pl.when(row >= shift)
        def _():
            fringe(comp).start()

    @pl.when(row >= fringes)
    def _():
        for comp in range(comps):
            field[0, comp, 2 : width + 2, :depth, :levels] = farm[comp].reshape(
                width, depth, levels
            )

    @pl.when(row < fringes)
    def _():
        for comp in range(comps):
            fringe(comp).wait_recv()

    for section, (weight, fresh_weight) in enumerate(WEIGHTS):
        for side, start in ((0, 0), (1, depth - 2)):
            edge[section, side] = field[section, :, 2 : width + 2, start : start + 2, :]
        copies = halo_copies(
            row, column, across, spanwise, section, field, edge, edge_in, halo_sem
        )
        for copy in copies:
            copy.start()
        drag_force(
            field[section, 0, 2 : width + 2, :depth, :].reshape(area, lanes),
            one_row, one_level, one_turb, force,
        )

        def landed(first, last, spans):
            for copy in copies[first:last]:
                copy.wait_recv()
            for low, high in spans:
                for comp in range(comps):
                    field[section, comp, low:high, depth : depth + 2, :] = edge_in[
                        section, 1, comp, low:high
                    ]
                    field[section, comp, low:high, 2 * depth - 2 :, :] = edge_in[
                        section, 0, comp, low:high
                    ]

        landed(0, 2, ((2, width + 2),))
        rest = functools.partial(
            landed, 2, len(SIDES), ((0, 2), (width + 2, width + 4))
        )
        final = section == len(WEIGHTS) - 1
        rate_section(
            levels, field.at[section], field.at[0], eddy, force, weight, fresh_weight,
            farm_out if final else field.at[section + 1], final, rest,
        )
        for copy in copies:
            copy.wait_send()

    @pl.when(row >= shift)
    def _():
        for comp in range(comps):
            fringe(comp).wait_send()


def shards(farm_velocity, precursor_velocity, turb_cell, turb_slot, disk_mask):
    across = lax.axis_size("gx")
    spanwise = lax.axis_size("gy")
    comps, width, depth, levels = precursor_velocity.shape
    count = across * spanwise
    area = width * depth
    lanes = -(-(levels + 2) // 128) * 128
    slots = turb_cell.shape[-1]
    tables = spectral_tables(across, spanwise, width, depth, levels, lanes)
    messages = comps * -(-levels // count)
    sections = len(WEIGHTS)
    vmem = pl.BlockSpec(memory_space=pltpu.VMEM)
    smem = pl.BlockSpec(memory_space=pltpu.SMEM)
    buffer = pltpu.VMEM((count, messages, area), jnp.float32)
    edges = pltpu.VMEM((sections, 2, comps, width, 2, lanes), jnp.float32)
    edges_in = pltpu.VMEM((sections, 2, comps, width + 4, 2, lanes), jnp.float32)
    field = jax.ShapeDtypeStruct((comps, area, levels), jnp.float32)
    farm_new, fresh = pl.pallas_call(
        functools.partial(step_body, across, spanwise),
        out_shape=(field, field),
        in_specs=[vmem] * 12 + [smem],
        out_specs=(vmem, vmem),
        scratch_shapes=[
            buffer,
            buffer,
            buffer,
            buffer,
            pltpu.VMEM((sections, comps, width + 4, 2 * depth, lanes), jnp.float32),
            pltpu.VMEM((width + 2, 2 * depth, lanes), jnp.float32),
            pltpu.VMEM((width, depth, lanes), jnp.float32),
            edges,
            edges_in,
            pltpu.VMEM((comps, width, depth, lanes), jnp.float32),
            pltpu.VMEM((area, slots), jnp.bfloat16),
            pltpu.VMEM((lanes, slots), jnp.float32),
            pltpu.VMEM((TURB, slots), jnp.float32),
            pltpu.SemaphoreType.DMA((2, count)),
            pltpu.SemaphoreType.DMA((2, count)),
            pltpu.SemaphoreType.DMA((2, comps)),
            pltpu.SemaphoreType.DMA((2, sections, len(SIDES))),
        ],
        compiler_params=pltpu.CompilerParams(collective_id=0, has_side_effects=True),
        name="farm_step",
    )(
        farm_velocity.reshape(field.shape),
        precursor_velocity.reshape(field.shape),
        turb_cell.reshape(1, slots),
        turb_slot.reshape(1, slots),
        disk_mask.reshape(1, slots),
        *[jnp.asarray(table) for table in tables],
    )
    return (farm_new.reshape(farm_velocity.shape), fresh.reshape(farm_velocity.shape))


def solution(mesh):
    return jax.shard_map(
        shards,
        mesh=mesh,
        in_specs=(
            P(None, "gx", "gy", None),
            P(None, "gx", "gy", None),
            P("gx", "gy", None),
            P("gx", "gy", None),
            P("gx", "gy", None),
        ),
        out_specs=(P(None, "gx", "gy", None), P(None, "gx", "gy", None)),
        check_vma=False,
    )
```
